256 devices in a mesh: dp: 4 (over x), tensor: 64 (over y, z, core).
Axes of the slice: x: 4, y: 4, z: 8, core: 2. Of those that a mesh axis runs over, the one named last changes fastest.
Arguments:
- query: bfloat16 [128, 16384], P('dp', 'tensor'), may hold values from -7.5 to 7.5
- cache_keys: bfloat16 [128, 32768, 128], P('dp', 'tensor'), may hold values from -3 to 3
- cache_values: bfloat16 [128, 32768, 128], P('dp', 'tensor'), may hold values from -5 to 5
- new_key: bfloat16 [128, 1024], P('dp'), may hold values from -5 to 5
- new_value: bfloat16 [128, 1024], P('dp'), may hold values from -5 to 5
- lengths: int32 [128], P('dp'), may hold values from 2 to 4096, as said below
- positions: int32 [128], P('dp'), may hold values from 4096 to 8191
- out_weight: bfloat16 [16384, 16384], P('tensor', 'dp'), may hold values from -0.375 to 0.375
- residual: bfloat16 [128, 16384], P('tensor', 'dp'), may hold values from -43 to 43
- norm_gain: bfloat16 [16384], P('dp'), may hold values from 0.5 to 1.5
Outputs:
- normed: bfloat16 [128, 16384], P('tensor', 'dp')
- stream: bfloat16 [128, 16384], P('tensor', 'dp')
The draws below stay inside these ranges and needn't reach their ends.
Inputs may be any that keep to these rules, and one draw needn't show every extreme that they name: `lengths`: every row keeps its first two slots; some row uses all 4096 slots and some row only two.
All inputs are finite; a program needn't handle non-finite values.
Results may differ from the reference program's by a relative error of at most 0.01.
Values may be sent and summed in bfloat16 or wider, within the bound.
A program may use at most 64 MiB of HBM per device.

```python
import math
import jax
import jax.numpy as jnp
from jax import lax

D = 16384
H = 128
KVH = 8
HD = 128
LEN = 4096
ROWS = 128


def draw_query(key, part):
    values = jnp.clip(jax.random.normal(jax.random.fold_in(key, 1), (ROWS, H, HD), jnp.float32), -4.0, 4.0)
    return values.reshape(ROWS, H * HD).astype(jnp.bfloat16)


def draw_cache_keys(key, part):
    values = jnp.clip(jax.random.normal(jax.random.fold_in(key, 2), (ROWS, KVH, LEN, HD), jnp.float32), -3.0, 3.0)
    return values.reshape(ROWS, KVH * LEN, HD).astype(jnp.bfloat16)


def draw_lengths(key, part):
    counts = jax.random.randint(jax.random.fold_in(key, 31), (ROWS,), 2, LEN + 1)
    longest = jax.random.randint(jax.random.fold_in(key, 32), (), 0, ROWS)
    shortest = (longest + 1 + jax.random.randint(jax.random.fold_in(key, 33), (), 0, ROWS - 1)) % ROWS
    counts = counts.at[longest].set(LEN)
    counts = counts.at[shortest].set(2)
    return counts.astype(jnp.int32)


def draw_residual(key, part):
    row_scale = jnp.exp(jax.random.uniform(jax.random.fold_in(key, 21), (ROWS, 1), jnp.float32, 0.0, math.log(10.0)))
    column_scale = jnp.exp(jax.random.uniform(jax.random.fold_in(key, 22), (1, D), jnp.float32, 0.0, math.log(10.0)))
    column_scale = column_scale * (1.0 + 0.75 * jnp.arange(D, dtype=jnp.float32)[None, :] / D)
    noise = jnp.clip(jax.random.normal(jax.random.fold_in(key, 23), (ROWS, D), jnp.float32), -4.0, 4.0)
    values = 0.05 * row_scale * column_scale * noise
    return values.astype(jnp.bfloat16)


def with_ends(entries, rng, smallest, top_value):
    spot = [jax.random.randint(jax.random.fold_in(rng, axis), (), 0, length) for axis, length in enumerate(entries.shape)]
    main_axis = entries.shape.index(max(entries.shape))
    next_to = spot[:main_axis] + [(spot[main_axis] + 1) % entries.shape[main_axis]] + spot[main_axis + 1:]
    return entries.at[tuple(spot)].set(smallest).at[tuple(next_to)].set(top_value)


def steps_of(rng, dims, split, least, top_value):
    level = 1.0
    for position, parts in split:
        steps = jax.random.uniform(jax.random.fold_in(jax.random.fold_in(rng, 6), position), (parts,), jnp.float32, least / len(split), top_value / len(split))
        level = level * jnp.repeat(jnp.exp(steps), dims[position] // parts).reshape((-1,) + (1,) * (len(dims) - 1 - position))
    return level


def scatter_about(stream_key, dims, scale, bound, pieces=(), kind=jnp.bfloat16):
    factor_of = steps_of(stream_key, dims, pieces, -0.22, 0.18) if pieces else 1.0
    values = jax.random.normal(stream_key, dims, jnp.float32) * scale * factor_of
    return jnp.minimum(jnp.maximum(values, -bound), bound).astype(kind)


def setup_inputs(seed: int = 0) -> dict:
    seeds = jax.random.split(jax.random.key(seed), 11)
    query = draw_query(jax.random.fold_in(seeds[10], 71), 0)
    cache_keys = draw_cache_keys(jax.random.fold_in(seeds[10], 71), 0)
    cache_values = scatter_about(seeds[2], (ROWS, KVH * LEN, HD), 1.0, 5.0, ((0, 4), (1, 64)))
    new_key = scatter_about(seeds[3], (ROWS, KVH * HD), 1.0, 5.0, ((0, 4),))
    new_value = scatter_about(seeds[4], (ROWS, KVH * HD), 1.0, 5.0, ((0, 4),))
    lengths = draw_lengths(jax.random.fold_in(seeds[10], 71), 0)
    positions = with_ends(jax.random.randint(seeds[6], (ROWS,), LEN, 2 * LEN), jax.random.fold_in(seeds[6], 1), LEN, (2 * LEN) - 1).astype(jnp.int32)
    out_weight = scatter_about(seeds[7], (H * HD, D), (H * 2) ** -0.5, 0.375, ((0, 64), (1, 4)))
    residual = draw_residual(jax.random.fold_in(seeds[10], 71), 0)
    norm_gain = jnp.clip(1.0 + 0.1 * jax.random.normal(seeds[9], (D,), jnp.float32), 0.5, 1.5).astype(jnp.bfloat16)
    return dict(query=query, cache_keys=cache_keys, cache_values=cache_values, new_key=new_key, new_value=new_value, lengths=lengths, positions=positions, out_weight=out_weight, residual=residual, norm_gain=norm_gain)


NEG_FILL = -1e+30

def rotate_keys(keys, positions):
    half_dim = keys.shape[-1] // 2
    frequency = 500000.0 ** (-(jnp.arange(half_dim, dtype=jnp.float32) * 2.0 / keys.shape[-1]))
    angles = positions.astype(jnp.float32)[:, None] * frequency[None, :]
    cosine = jnp.cos(angles)[:, None, :]
    sine_part = jnp.sin(angles)[:, None, :]
    first_half = keys[..., :half_dim]
    second_half = keys[..., half_dim:]
    return jnp.concatenate([first_half * cosine - second_half * sine_part, second_half * cosine + first_half * sine_part], axis=-1)

def attend_row(packed):
    query_row, key_row, value_row, new_key_row, new_value_row, length = packed
    per_group = H // KVH
    query_heads = jnp.transpose(query_row.reshape(per_group, KVH, HD), (1, 0, 2)).astype(jnp.float32)
    key_heads = key_row.reshape(KVH, LEN, HD).astype(jnp.float32)
    value_heads = value_row.reshape(KVH, LEN, HD).astype(jnp.float32)
    inv_root = 1.0 / math.sqrt(HD)
    scores = jnp.einsum('ghd,gpd->ghp', query_heads, key_heads) * inv_root
    in_cache = (jnp.arange(LEN, dtype=jnp.int32) < length)[None, None, :]
    scores = jnp.where(in_cache, scores, NEG_FILL)
    fresh = jnp.einsum('ghd,gd->gh', query_heads, new_key_row.astype(jnp.float32)) * inv_root
    top = jnp.maximum(lax.optimization_barrier(jnp.max(scores, axis=-1)), fresh)
    weights = jnp.where(in_cache, jnp.exp(scores - top[..., None]), 0.0)
    fresh_weight = jnp.exp(fresh - top)
    weight_sum = lax.optimization_barrier(jnp.sum(weights, axis=-1)) + fresh_weight
    rounded = lax.optimization_barrier(weights.astype(jnp.bfloat16)).astype(jnp.float32)
    numerator = jnp.einsum('ghp,gpd->ghd', rounded, value_heads)
    numerator = numerator + fresh_weight[..., None] * new_value_row.astype(jnp.float32)[:, None, :]
    return (numerator / weight_sum[..., None]).astype(jnp.bfloat16).reshape(H * HD)

def reference(query, cache_keys, cache_values, new_key, new_value, lengths, positions, out_weight, residual, norm_gain):
    rotated = rotate_keys(new_key.reshape(ROWS, KVH, HD).astype(jnp.float32), positions).astype(jnp.bfloat16)
    attended = lax.map(attend_row, (query, cache_keys, cache_values, rotated, new_value.reshape(ROWS, KVH, HD), lengths))
    projected = jnp.dot(attended, out_weight, preferred_element_type=jnp.float32)
    hidden_sum = residual.astype(jnp.float32) + projected
    stream = hidden_sum.astype(jnp.bfloat16)
    mean_square = lax.optimization_barrier(jnp.mean(hidden_sum * hidden_sum, axis=-1, keepdims=True))
    normed = (hidden_sum * lax.rsqrt(mean_square + 1e-05) * norm_gain.astype(jnp.float32)).astype(jnp.bfloat16)
    return (normed, stream)
```

```python
import math

import jax
import jax.numpy as jnp
from jax import lax
from jax.experimental import pallas as pl
from jax.experimental.pallas import tpu as pltpu
from jax.sharding import PartitionSpec as P

D = 16384
NEG_FILL = -1e30
MESH = pl.DeviceIdType.MESH
LOG_BASE = math.log(500000.0)
F32 = jnp.float32
BF16 = jnp.bfloat16
NY, NZ = 4, 8
CH = 512
NCH = 4


def kernel(
    len_ref, pos_ref, q_ref, k_ref, v_ref, nk_ref, nv_ref, w_ref, res_ref, gain_ref,
    normed_ref, stream_ref,
    kbuf, vbuf, wbuf, nkbuf, nvbuf, resbuf, gainbuf, krotbuf, nvf,
    q1buf, q2buf, qf, accf, accb, statb, cbuf, sbuf, attbuf,
    psend, precv, ysend, yrecv, zf, zsend, zrecv, sf, sqsend, sqrecv,
    lsem, ssem, q1sem, q2sem, csem, tsem, dsem, psem, ysem, zsem, qsem,
):
    x = lax.axis_index("dp")
    t = lax.axis_index("tensor")
    c = lax.rem(t, 2)
    z = lax.rem(t // 2, NZ)
    y = t // (2 * NZ)
    g = t // 8
    b = lax.rem(t, 8)
    gpar = lax.rem(g, 2)
    tt = lax.rem(t, 16)

    def dev(yy, zz, cc):
        return (yy * NZ + zz) * 2 + cc

    loads = []

    def load(src, dst):
        cp = pltpu.make_async_copy(src, dst, lsem.at[len(loads)])
        cp.start()
        loads.append(cp)
        return cp

    small = [
        load(nk_ref.at[:, pl.ds(pl.multiple_of(g * 128, 128), 128)], nkbuf),
        load(nv_ref.at[:, pl.ds(pl.multiple_of(g * 128, 128), 128)], nvbuf),
    ]
    kload = [load(k_ref.at[pl.ds(8 * i, 8)], kbuf.at[pl.ds(8 * i, 8)]) for i in range(4)]
    vload = [load(v_ref.at[pl.ds(8 * i, 8)], vbuf.at[pl.ds(8 * i, 8)]) for i in range(4)]
    wload = [load(w_ref.at[pl.ds(64 * i, 64)], wbuf.at[pl.ds(64 * i, 64)]) for i in range(4)]
    late = [load(res_ref, resbuf), load(gain_ref, gainbuf)]

    barrier = pltpu.get_barrier_semaphore()
    partners = []
    for d in range(1, 16):
        partners.append((x, y * 16 + lax.rem(tt + d, 16)))
    for d in range(1, NY):
        for cc in range(2):
            partners.append((x, dev(lax.rem(y + d, NY), z, cc)))
    for d in range(1, 4):
        partners.append((lax.rem(x + d, 4), t))
    for px, pt in partners:
        pl.semaphore_signal(barrier, inc=1, device_id=(px, pt), device_id_type=MESH)
    pl.semaphore_wait(barrier, len(partners))

    sends = []
    counter = [0]

    def remote(src, dst, rsem, pt, px=x, keep=True):
        cp = pltpu.make_async_remote_copy(
            src_ref=src, dst_ref=dst, send_sem=ssem.at[counter[0]], recv_sem=rsem,
            device_id=(px, pt), device_id_type=MESH,
        )
        counter[0] += 1
        if keep:
            cp.start()
            sends.append(cp)
        return cp

    def arrived(ref, sem):
        pltpu.make_async_copy(ref, ref, sem).wait()

    ydest = 2 * lax.rem(z, 2) + c
    q1 = []
    for half in range(2):
        target = dev(ydest, z, half)
        src = q_ref.at[:, half * 128:(half + 1) * 128]
        dst = q1buf.at[y]
        cp = remote(src, dst, q1sem.at[y], target, keep=False)
        here = jnp.logical_and(ydest == y, c == half)
        mine = pltpu.make_async_copy(src, dst, q1sem.at[y])
        q1.append((cp, here))

        @pl.when(here)
        def _():
            mine.start()

        @pl.when(jnp.logical_not(here))
        def _():
            cp.start()

    relay = lax.rem(z, 2) == y // 2
    slot = z // 2
    q2 = []
    for i in range(4):
        for cc in range(2):
            zz = 4 * c + lax.rem(z + i, 4)
            target = dev(y, zz, cc)
            cp = remote(q1buf, q2buf.at[slot], q2sem.at[slot], target, keep=False)
            here = jnp.logical_and(zz == z, c == cc)
            mine = pltpu.make_async_copy(q1buf, q2buf.at[slot], q2sem.at[slot])
            q2.append((cp, mine, here))

    @pl.when(relay)
    def _():
        for i in range(NY):
            arrived(q1buf.at[i], q1sem.at[i])
        for cp, mine, here in q2:
            @pl.when(here)
            def _():
                mine.start()

            @pl.when(jnp.logical_not(here))
            def _():
                cp.start()

    for cp in small:
        cp.wait()
    row_ids = lax.broadcasted_iota(jnp.int32, (32, 128), 0)
    lane_ids = lax.broadcasted_iota(jnp.int32, (32, 128), 1)
    pos = jnp.zeros((32, 128), jnp.int32)
    for r in range(32):
        pos = jnp.where(row_ids == r, pos_ref[r], pos)
    j = jnp.where(lane_ids < 64, lane_ids, lane_ids - 64).astype(F32)
    frequency = jnp.exp(-(j * (2.0 / 128.0)) * LOG_BASE)
    angle = pos.astype(F32) * frequency
    cosine = jnp.cos(angle)
    sine = jnp.sin(angle)
    fresh_key = nkbuf[...].astype(F32)
    swapped = pltpu.roll(fresh_key, 64, 1)
    signed = jnp.where(lane_ids < 64, -sine, sine)
    krotbuf[...] = (fresh_key * cosine + swapped * signed).astype(BF16).astype(F32)
    nvf[...] = nvbuf[...].astype(F32)

    for cp in kload + vload:
        cp.wait()
    for i in range(4):
        arrived(q2buf.at[i], q2sem.at[i])
    for i in range(4):
        for ys in range(NY):
            qf[:, 4 * ys + i, :] = q2buf[i, ys].astype(F32)

    inv_root = 1.0 / math.sqrt(128.0)
    slot_ids = b * 512 + lax.broadcasted_iota(jnp.int32, (16, 512), 1)
    stat_lane = lax.broadcasted_iota(jnp.int32, (16, 128), 1)
    holder = b == 0
    stats = jnp.zeros((16, 128), F32)
    for ch in range(2):
        def group(i, stats, ch=ch):
            base = (ch * 2 + i) * 8
            for u in range(8):
                r = base + u
                qrow = qf[r]
                used = slot_ids < len_ref[r]
                score = lax.dot_general(
                    qrow.astype(BF16), kbuf[r], (((1,), (1,)), ((), ())),
                    preferred_element_type=F32,
                ) * inv_root
                score = jnp.where(used, score, NEG_FILL)
                fresh = jnp.sum(qrow * krotbuf[pl.ds(r, 1), :], axis=1, keepdims=True) * inv_root
                fresh = jnp.where(holder, fresh, NEG_FILL)
                top = jnp.maximum(jnp.max(score, axis=1, keepdims=True), fresh)
                weight = jnp.where(used, jnp.exp(score - top), 0.0)
                fresh_weight = jnp.where(holder, jnp.exp(fresh - top), 0.0)
                total = jnp.sum(weight, axis=1, keepdims=True) + fresh_weight
                acc = jnp.dot(weight.astype(BF16), vbuf[r], preferred_element_type=F32)
                acc = acc + fresh_weight * nvf[pl.ds(r, 1), :]
                accf[i, :, u, :] = acc
                stats = jnp.where(stat_lane == r, top, stats)
                stats = jnp.where(stat_lane == r + 64, total, stats)
            return stats

        stats = lax.fori_loop(0, 2, group, stats)
        merged = jnp.concatenate([accf[0], accf[1]], axis=1).astype(BF16)
        accb[ch] = merged.reshape(8, 2, 16, 128)
        if ch == 1:
            for o in range(8):
                statb[o] = stats[2 * o:2 * o + 2]
        for d in range(1, 8):
            o = lax.rem(b + d, 8)
            remote(accb.at[ch, o], cbuf.at[ch, d], csem.at[ch, d], g * 8 + o)
            if ch == 1:
                remote(statb.at[o], sbuf.at[d], tsem.at[d], g * 8 + o)
        cbuf[ch, 0] = accb[ch, b]
    sbuf[0] = statb[b]

    for d in range(1, 8):
        arrived(sbuf.at[d], tsem.at[d])
    rows = [sbuf[d] for d in range(8)]
    stacked = jnp.concatenate(
        [row[0:1] for row in rows] + [row[1:2] for row in rows], axis=0
    )
    turned = stacked.T
    for d in range(1, 8):
        arrived(cbuf.at[0, d], csem.at[0, d])
        arrived(cbuf.at[1, d], csem.at[1, d])
    for h in range(2):
        tops = turned[0:32, h * 8:h * 8 + 8]
        sums = turned[64:96, h * 8:h * 8 + 8]
        top = jnp.max(tops, axis=1, keepdims=True)
        scale = jnp.exp(tops - top)
        scale = scale / jnp.sum(scale * sums, axis=1, keepdims=True)
        total = jnp.zeros((32, 128), F32)
        for d in range(8):
            part = jnp.concatenate([cbuf[0, d, h], cbuf[1, d, h]], axis=0).astype(F32)
            total = total + part * scale[:, d:d + 1]
        attbuf[x, :, h * 128:(h + 1) * 128] = total.astype(BF16)

    for d in range(1, 4):
        remote(attbuf.at[x], attbuf.at[x], dsem.at[x], t, px=lax.rem(x + d, 4))
    for cp in wload:
        cp.wait()
    for d in range(1, 4):
        o = lax.rem(x + d, 4)
        arrived(attbuf.at[o], dsem.at[o])
    att = attbuf[...].reshape(128, 256)

    pair = dev(y, z, 1 - c)
    for i in range(NCH):
        start = pl.multiple_of((1 - c) * (NCH * CH) + i * CH, CH)
        psend[i] = jnp.dot(att, wbuf[:, pl.ds(start, CH)], preferred_element_type=F32).astype(BF16)
        remote(psend.at[i], precv.at[i], psem.at[i], pair)
    for i in range(NCH):
        start = pl.multiple_of(c * (NCH * CH) + i * CH, CH)
        own = jnp.dot(att, wbuf[:, pl.ds(start, CH)], preferred_element_type=F32)
        arrived(precv.at[i], psem.at[i])
        ysend[i] = (own + precv[i].astype(F32)).astype(BF16).reshape(NY, 32, CH)
        for d in (2, 1, 3):
            o = lax.rem(y + d, NY)
            remote(ysend.at[i, o], yrecv.at[i, d - 1], ysem.at[i, d - 1], dev(o, z, c))

    for p in range(2):
        for k in range(2):
            i = 2 * p + k
            for d in range(1, NY):
                arrived(yrecv.at[i, d - 1], ysem.at[i, d - 1])
            summed = ysend[i, y].astype(F32)
            for d in range(1, NY):
                summed = summed + yrecv[i, d - 1].astype(F32)
            for cb in range(4):
                zf[:, 4 * k + cb, :] = summed[:, cb * 128:(cb + 1) * 128]
        zsend[p] = zf[...].astype(BF16).reshape(16, 2, 8, 128)
        for d in (8, 7, 9, 6, 10, 5, 11, 4, 12, 3, 13, 2, 14, 1, 15):
            o = lax.rem(tt + d, 16)
            remote(zsend.at[p, o], zrecv.at[p, d], zsem.at[p, d], y * 16 + o)
        zrecv[p, 0] = zsend[p, tt]
    for cp in late:
        cp.wait()
    for p in range(2):
        for d in range(1, 16):
            arrived(zrecv.at[p, d], zsem.at[p, d])
        for parity in range(2):
            total = zrecv[p, parity].astype(F32)
            for d in range(parity + 2, 16, 2):
                total = total + zrecv[p, d].astype(F32)
            half = c if parity == 0 else 1 - c
            for row in range(2):
                sf[row, half, p * 8:(p + 1) * 8, :] = total[row]
    hidden = jnp.concatenate(
        [sf[:, half, cb, :] for half in range(2) for cb in range(16)], axis=1
    )
    hidden = resbuf[...].astype(F32) + hidden
    stream_ref[...] = hidden.astype(BF16)
    squares = jnp.sum(hidden * hidden, axis=1, keepdims=True)
    sqsend[...] = jnp.broadcast_to(squares, (2, 128))
    for d in range(1, 4):
        remote(sqsend, sqrecv.at[d - 1], qsem.at[d - 1], t, px=lax.rem(x + d, 4))
    for d in range(1, 4):
        arrived(sqrecv.at[d - 1], qsem.at[d - 1])
    whole = sqsend[...]
    for d in range(3):
        whole = whole + sqrecv[d]
    factor = lax.rsqrt(whole[:, 0:1] / D + 1e-05)
    normed_ref[...] = (hidden * factor * gainbuf[...].astype(F32)).astype(BF16)

    for cp, here in q1:
        @pl.when(jnp.logical_not(here))
        def _():
            cp.wait_send()

    @pl.when(relay)
    def _():
        for cp, mine, here in q2:
            @pl.when(jnp.logical_not(here))
            def _():
                cp.wait_send()
    for cp in sends:
        cp.wait_send()


def local(query, cache_keys, cache_values, new_key, new_value, lengths, positions, out_weight, residual, norm_gain):
    any_spec = pl.BlockSpec(memory_space=pl.ANY)
    smem = pl.BlockSpec(memory_space=pltpu.SMEM)
    vmem = pl.BlockSpec(memory_space=pltpu.VMEM)
    dma = pltpu.SemaphoreType.DMA
    normed, stream = pl.pallas_call(
        kernel,
        out_shape=(
            jax.ShapeDtypeStruct((2, 4096), BF16),
            jax.ShapeDtypeStruct((2, 4096), BF16),
        ),
        in_specs=[smem, smem] + [any_spec] * 8,
        out_specs=(vmem, vmem),
        scratch_shapes=[
            pltpu.VMEM((32, 512, 128), BF16),
            pltpu.VMEM((32, 512, 128), BF16),
            pltpu.VMEM((256, 4096), BF16),
            pltpu.VMEM((32, 128), BF16),
            pltpu.VMEM((32, 128), BF16),
            pltpu.VMEM((2, 4096), BF16),
            pltpu.VMEM((1, 4096), BF16),
            pltpu.VMEM((32, 128), F32),
            pltpu.VMEM((32, 128), F32),
            pltpu.VMEM((4, 32, 128), BF16),
            pltpu.VMEM((4, 4, 32, 128), BF16),
            pltpu.VMEM((32, 16, 128), F32),
            pltpu.VMEM((2, 16, 8, 128), F32),
            pltpu.VMEM((2, 8, 2, 16, 128), BF16),
            pltpu.VMEM((8, 2, 128), F32),
            pltpu.VMEM((2, 8, 2, 16, 128), BF16),
            pltpu.VMEM((8, 2, 128), F32),
            pltpu.VMEM((4, 32, 256), BF16),
            pltpu.VMEM((NCH, 128, CH), BF16),
            pltpu.VMEM((NCH, 128, CH), BF16),
            pltpu.VMEM((NCH, 4, 32, CH), BF16),
            pltpu.VMEM((NCH, 3, 32, CH), BF16),
            pltpu.VMEM((32, 8, 128), F32),
            pltpu.VMEM((2, 16, 2, 8, 128), BF16),
            pltpu.VMEM((2, 16, 2, 8, 128), BF16),
            pltpu.VMEM((2, 2, 16, 128), F32),
            pltpu.VMEM((2, 128), F32),
            pltpu.VMEM((3, 2, 128), F32),
            dma((16,)),
            dma((96,)),
            dma((4,)),
            dma((4,)),
            dma((2, 8)),
            dma((8,)),
            dma((4,)),
            dma((NCH,)),
            dma((NCH, 3)),
            dma((2, 16)),
            dma((3,)),
        ],
        compiler_params=pltpu.CompilerParams(
            collective_id=0, has_side_effects=True, vmem_limit_bytes=60 * 1024 * 1024
        ),
    )(
        lengths, positions, query, cache_keys, cache_values, new_key, new_value,
        out_weight, residual, norm_gain.reshape(1, -1),
    )
    return normed, stream


def solution(mesh):
    placed = (
        P("dp", "tensor"),
        P("dp", "tensor", None),
        P("dp", "tensor", None),
        P("dp", None),
        P("dp", None),
        P("dp"),
        P("dp"),
        P("tensor", "dp"),
        P("tensor", "dp"),
        P("dp"),
    )
    return jax.shard_map(
        local,
        mesh=mesh,
        in_specs=placed,
        out_specs=(P("tensor", "dp"), P("tensor", "dp")),
        check_vma=False,
    )
```

```python
import math

import jax
import jax.numpy as jnp
from jax import lax
from jax.experimental import pallas as pl
from jax.experimental.pallas import tpu as pltpu
from jax.sharding import PartitionSpec as P

D = 16384
NEG_FILL = -1e30
MESH = pl.DeviceIdType.MESH
LOG_BASE = math.log(500000.0)
F32 = jnp.float32
BF16 = jnp.bfloat16
NY, NZ = 4, 8
CH = 512
NCH = 4


def kernel(
    len_ref, pos_ref, q_ref, k_ref, v_ref, nk_ref, nv_ref, w_ref, res_ref, gain_ref,
    normed_ref, stream_ref,
    kbuf, vbuf, wbuf, nkbuf, nvbuf, resbuf, gainbuf, krotbuf, nvf,
    q1buf, q2buf, qf, accf, accb, statb, cbuf, sbuf, attbuf,
    ysend, yrecv, zf, zsend, zrecv, sf, sqsend, sqrecv,
    lsem, ssem, wsem, q1sem, q2sem, csem, tsem, dsem, ysem, zsem, qsem,
):
    x = lax.axis_index("dp")
    t = lax.axis_index("tensor")
    c = lax.rem(t, 2)
    z = lax.rem(t // 2, NZ)
    y = t // (2 * NZ)
    g = t // 8
    b = lax.rem(t, 8)
    gpar = lax.rem(g, 2)
    tt = lax.rem(t, 16)

    def dev(yy, zz, cc):
        return (yy * NZ + zz) * 2 + cc

    loads = []

    def load(src, dst):
        cp = pltpu.make_async_copy(src, dst, lsem.at[len(loads)])
        cp.start()
        loads.append(cp)
        return cp

    small = [
        load(nk_ref.at[:, pl.ds(pl.multiple_of(g * 128, 128), 128)], nkbuf),
        load(nv_ref.at[:, pl.ds(pl.multiple_of(g * 128, 128), 128)], nvbuf),
    ]
    kload = [load(k_ref.at[pl.ds(8 * i, 8)], kbuf.at[pl.ds(8 * i, 8)]) for i in range(4)]
    vload = [load(v_ref.at[pl.ds(8 * i, 8)], vbuf.at[pl.ds(8 * i, 8)]) for i in range(4)]
    mycols = pl.ds(pl.multiple_of(c * (NCH * CH), NCH * CH), NCH * CH)
    theircols = pl.ds(pl.multiple_of((1 - c) * (NCH * CH), NCH * CH), NCH * CH)
    wload = [
        load(w_ref.at[pl.ds(64 * i, 64), mycols], wbuf.at[c, pl.ds(64 * i, 64)]) for i in range(4)
    ]
    late = [load(res_ref, resbuf), load(gain_ref, gainbuf)]

    barrier = pltpu.get_barrier_semaphore()
    partners = []
    for d in range(1, 16):
        partners.append((x, y * 16 + lax.rem(tt + d, 16)))
    for d in range(1, NY):
        for cc in range(2):
            partners.append((x, dev(lax.rem(y + d, NY), z, cc)))
    for d in range(1, 4):
        for cc in range(2):
            partners.append((lax.rem(x + d, 4), dev(y, z, cc)))
    for px, pt in partners:
        pl.semaphore_signal(barrier, inc=1, device_id=(px, pt), device_id_type=MESH)
    pl.semaphore_wait(barrier, len(partners))

    sends = []
    counter = [0]

    def remote(src, dst, rsem, pt, px=x, keep=True):
        cp = pltpu.make_async_remote_copy(
            src_ref=src, dst_ref=dst, send_sem=ssem.at[counter[0]], recv_sem=rsem,
            device_id=(px, pt), device_id_type=MESH,
        )
        counter[0] += 1
        if keep:
            cp.start()
            sends.append(cp)
        return cp

    def arrived(ref, sem):
        pltpu.make_async_copy(ref, ref, sem).wait()

    ydest = 2 * lax.rem(z, 2) + c
    q1 = []
    for half in range(2):
        target = dev(ydest, z, half)
        src = q_ref.at[:, half * 128:(half + 1) * 128]
        dst = q1buf.at[y]
        cp = remote(src, dst, q1sem.at[y], target, keep=False)
        here = jnp.logical_and(ydest == y, c == half)
        mine = pltpu.make_async_copy(src, dst, q1sem.at[y])
        q1.append((cp, here))

        @pl.when(here)
        def _():
            mine.start()

        @pl.when(jnp.logical_not(here))
        def _():
            cp.start()

    relay = lax.rem(z, 2) == y // 2
    slot = z // 2
    q2 = []
    for i in range(4):
        for cc in range(2):
            zz = 4 * c + lax.rem(z + i, 4)
            target = dev(y, zz, cc)
            cp = remote(q1buf, q2buf.at[slot], q2sem.at[slot], target, keep=False)
            here = jnp.logical_and(zz == z, c == cc)
            mine = pltpu.make_async_copy(q1buf, q2buf.at[slot], q2sem.at[slot])
            q2.append((cp, mine, here))

    @pl.when(relay)
    def _():
        for i in range(NY):
            arrived(q1buf.at[i], q1sem.at[i])
        for cp, mine, here in q2:
            @pl.when(here)
            def _():
                mine.start()

            @pl.when(jnp.logical_not(here))
            def _():
                cp.start()

    for i in range(4):
        remote(
            w_ref.at[pl.ds(64 * i, 64), theircols], wbuf.at[c, pl.ds(64 * i, 64)],
            wsem.at[i], dev(y, z, 1 - c),
        )

    for cp in small:
        cp.wait()
    row_ids = lax.broadcasted_iota(jnp.int32, (32, 128), 0)
    lane_ids = lax.broadcasted_iota(jnp.int32, (32, 128), 1)
    pos = jnp.zeros((32, 128), jnp.int32)
    for r in range(32):
        pos = jnp.where(row_ids == r, pos_ref[r], pos)
    j = jnp.where(lane_ids < 64, lane_ids, lane_ids - 64).astype(F32)
    frequency = jnp.exp(-(j * (2.0 / 128.0)) * LOG_BASE)
    angle = pos.astype(F32) * frequency
    cosine = jnp.cos(angle)
    sine = jnp.sin(angle)
    fresh_key = nkbuf[...].astype(F32)
    swapped = pltpu.roll(fresh_key, 64, 1)
    signed = jnp.where(lane_ids < 64, -sine, sine)
    krotbuf[...] = (fresh_key * cosine + swapped * signed).astype(BF16).astype(F32)
    nvf[...] = nvbuf[...].astype(F32)

    for cp in kload + vload:
        cp.wait()
    for i in range(4):
        arrived(q2buf.at[i], q2sem.at[i])
    for i in range(4):
        for ys in range(NY):
            qf[:, 4 * ys + i, :] = q2buf[i, ys].astype(F32)

    inv_root = 1.0 / math.sqrt(128.0)
    slot_ids = b * 512 + lax.broadcasted_iota(jnp.int32, (16, 512), 1)
    stat_lane = lax.broadcasted_iota(jnp.int32, (16, 128), 1)
    holder = b == 0
    stats = jnp.zeros((16, 128), F32)
    for ch in range(2):
        def group(i, stats, ch=ch):
            base = (ch * 2 + i) * 8
            for u in range(8):
                r = base + u
                qrow = qf[r]
                used = slot_ids < len_ref[r]
                score = lax.dot_general(
                    qrow.astype(BF16), kbuf[r], (((1,), (1,)), ((), ())),
                    preferred_element_type=F32,
                ) * inv_root
                score = jnp.where(used, score, NEG_FILL)
                fresh = jnp.sum(qrow * krotbuf[pl.ds(r, 1), :], axis=1, keepdims=True) * inv_root
                fresh = jnp.where(holder, fresh, NEG_FILL)
                top = jnp.maximum(jnp.max(score, axis=1, keepdims=True), fresh)
                weight = jnp.where(used, jnp.exp(score - top), 0.0)
                fresh_weight = jnp.where(holder, jnp.exp(fresh - top), 0.0)
                total = jnp.sum(weight, axis=1, keepdims=True) + fresh_weight
                acc = jnp.dot(weight.astype(BF16), vbuf[r], preferred_element_type=F32)
                acc = acc + fresh_weight * nvf[pl.ds(r, 1), :]
                accf[i, :, u, :] = acc
                stats = jnp.where(stat_lane == r, top, stats)
                stats = jnp.where(stat_lane == r + 64, total, stats)
            return stats

        stats = lax.fori_loop(0, 2, group, stats)
        merged = jnp.concatenate([accf[0], accf[1]], axis=1).astype(BF16)
        accb[ch] = merged.reshape(8, 2, 16, 128)
        if ch == 1:
            for o in range(8):
                statb[o] = stats[2 * o:2 * o + 2]
        for d in range(1, 8):
            o = lax.rem(b + d, 8)
            remote(accb.at[ch, o], cbuf.at[ch, d], csem.at[ch, d], g * 8 + o)
            if ch == 1:
                remote(statb.at[o], sbuf.at[d], tsem.at[d], g * 8 + o)
        cbuf[ch, 0] = accb[ch, b]
    sbuf[0] = statb[b]

    for d in range(1, 8):
        arrived(sbuf.at[d], tsem.at[d])
    rows = [sbuf[d] for d in range(8)]
    stacked = jnp.concatenate(
        [row[0:1] for row in rows] + [row[1:2] for row in rows], axis=0
    )
    turned = stacked.T
    for d in range(1, 8):
        arrived(cbuf.at[0, d], csem.at[0, d])
        arrived(cbuf.at[1, d], csem.at[1, d])
    for h in range(2):
        tops = turned[0:32, h * 8:h * 8 + 8]
        sums = turned[64:96, h * 8:h * 8 + 8]
        top = jnp.max(tops, axis=1, keepdims=True)
        scale = jnp.exp(tops - top)
        scale = scale / jnp.sum(scale * sums, axis=1, keepdims=True)
        total = jnp.zeros((32, 128), F32)
        for d in range(8):
            part = jnp.concatenate([cbuf[0, d, h], cbuf[1, d, h]], axis=0).astype(F32)
            total = total + part * scale[:, d:d + 1]
        attbuf[c, x, :, h * 128:(h + 1) * 128] = total.astype(BF16)

    for d in (2, 1, 3, 0):
        o = lax.rem(x + d, 4)
        for cc in (c, 1 - c):
            if d > 0 or cc is not c:
                remote(attbuf.at[c, x], attbuf.at[c, x], dsem.at[c, x], dev(y, z, cc), px=o)
    for cp in wload:
        cp.wait()
    for i in range(4):
        arrived(wbuf.at[1 - c, pl.ds(64 * i, 64)], wsem.at[i])
    for d in (0, 1, 3, 2):
        o = lax.rem(x + d, 4)
        for cc in (c, 1 - c):
            if d > 0 or cc is not c:
                arrived(attbuf.at[cc, o], dsem.at[cc, o])
    att = jnp.concatenate([attbuf[0].reshape(128, 256), attbuf[1].reshape(128, 256)], axis=1)

    for i in range(NCH):
        own = jnp.dot(
            att, wbuf[:, :, i * CH:(i + 1) * CH].reshape(512, CH), preferred_element_type=F32
        )
        ysend[i] = own.astype(BF16).reshape(NY, 32, CH)
        for d in (2, 1, 3):
            o = lax.rem(y + d, NY)
            remote(ysend.at[i, o], yrecv.at[i, d - 1], ysem.at[i, d - 1], dev(o, z, c))

    for p in range(2):
        for k in range(2):
            i = 2 * p + k
            for d in range(1, NY):
                arrived(yrecv.at[i, d - 1], ysem.at[i, d - 1])
            summed = ysend[i, y].astype(F32)
            for d in range(1, NY):
                summed = summed + yrecv[i, d - 1].astype(F32)
            for cb in range(4):
                zf[:, 4 * k + cb, :] = summed[:, cb * 128:(cb + 1) * 128]
        zsend[p] = zf[...].astype(BF16).reshape(16, 2, 8, 128)
        for d in (8, 7, 9, 6, 10, 5, 11, 4, 12, 3, 13, 2, 14, 1, 15):
            o = lax.rem(tt + d, 16)
            remote(zsend.at[p, o], zrecv.at[p, d], zsem.at[p, d], y * 16 + o)
        zrecv[p, 0] = zsend[p, tt]
    for cp in late:
        cp.wait()
    for p in range(2):
        for d in range(1, 16):
            arrived(zrecv.at[p, d], zsem.at[p, d])
        for parity in range(2):
            total = zrecv[p, parity].astype(F32)
            for d in range(parity + 2, 16, 2):
                total = total + zrecv[p, d].astype(F32)
            half = c if parity == 0 else 1 - c
            for row in range(2):
                sf[row, half, p * 8:(p + 1) * 8, :] = total[row]
    hidden = jnp.concatenate(
        [sf[:, half, cb, :] for half in range(2) for cb in range(16)], axis=1
    )
    hidden = resbuf[...].astype(F32) + hidden
    stream_ref[...] = hidden.astype(BF16)
    squares = jnp.sum(hidden * hidden, axis=1, keepdims=True)
    sqsend[...] = jnp.broadcast_to(squares, (2, 128))
    for d in range(1, 4):
        remote(sqsend, sqrecv.at[d - 1], qsem.at[d - 1], t, px=lax.rem(x + d, 4))
    for d in range(1, 4):
        arrived(sqrecv.at[d - 1], qsem.at[d - 1])
    whole = sqsend[...]
    for d in range(3):
        whole = whole + sqrecv[d]
    factor = lax.rsqrt(whole[:, 0:1] / D + 1e-05)
    normed_ref[...] = (hidden * factor * gainbuf[...].astype(F32)).astype(BF16)

    for cp, here in q1:
        @pl.when(jnp.logical_not(here))
        def _():
            cp.wait_send()

    @pl.when(relay)
    def _():
        for cp, mine, here in q2:
            @pl.when(jnp.logical_not(here))
            def _():
                cp.wait_send()
    for cp in sends:
        cp.wait_send()


def local(query, cache_keys, cache_values, new_key, new_value, lengths, positions, out_weight, residual, norm_gain):
    any_spec = pl.BlockSpec(memory_space=pl.ANY)
    smem = pl.BlockSpec(memory_space=pltpu.SMEM)
    vmem = pl.BlockSpec(memory_space=pltpu.VMEM)
    dma = pltpu.SemaphoreType.DMA
    normed, stream = pl.pallas_call(
        kernel,
        out_shape=(
            jax.ShapeDtypeStruct((2, 4096), BF16),
            jax.ShapeDtypeStruct((2, 4096), BF16),
        ),
        in_specs=[smem, smem] + [any_spec] * 8,
        out_specs=(vmem, vmem),
        scratch_shapes=[
            pltpu.VMEM((32, 512, 128), BF16),
            pltpu.VMEM((32, 512, 128), BF16),
            pltpu.VMEM((2, 256, NCH * CH), BF16),
            pltpu.VMEM((32, 128), BF16),
            pltpu.VMEM((32, 128), BF16),
            pltpu.VMEM((2, 4096), BF16),
            pltpu.VMEM((1, 4096), BF16),
            pltpu.VMEM((32, 128), F32),
            pltpu.VMEM((32, 128), F32),
            pltpu.VMEM((4, 32, 128), BF16),
            pltpu.VMEM((4, 4, 32, 128), BF16),
            pltpu.VMEM((32, 16, 128), F32),
            pltpu.VMEM((2, 16, 8, 128), F32),
            pltpu.VMEM((2, 8, 2, 16, 128), BF16),
            pltpu.VMEM((8, 2, 128), F32),
            pltpu.VMEM((2, 8, 2, 16, 128), BF16),
            pltpu.VMEM((8, 2, 128), F32),
            pltpu.VMEM((2, 4, 32, 256), BF16),
            pltpu.VMEM((NCH, 4, 32, CH), BF16),
            pltpu.VMEM((NCH, 3, 32, CH), BF16),
            pltpu.VMEM((32, 8, 128), F32),
            pltpu.VMEM((2, 16, 2, 8, 128), BF16),
            pltpu.VMEM((2, 16, 2, 8, 128), BF16),
            pltpu.VMEM((2, 2, 16, 128), F32),
            pltpu.VMEM((2, 128), F32),
            pltpu.VMEM((3, 2, 128), F32),
            dma((16,)),
            dma((112,)),
            dma((4,)),
            dma((4,)),
            dma((4,)),
            dma((2, 8)),
            dma((8,)),
            dma((2, 4)),
            dma((NCH, 3)),
            dma((2, 16)),
            dma((3,)),
        ],
        compiler_params=pltpu.CompilerParams(
            collective_id=0, has_side_effects=True, vmem_limit_bytes=60 * 1024 * 1024
        ),
    )(
        lengths, positions, query, cache_keys, cache_values, new_key, new_value,
        out_weight, residual, norm_gain.reshape(1, -1),
    )
    return normed, stream


def solution(mesh):
    placed = (
        P("dp", "tensor"),
        P("dp", "tensor", None),
        P("dp", "tensor", None),
        P("dp", None),
        P("dp", None),
        P("dp"),
        P("dp"),
        P("tensor", "dp"),
        P("tensor", "dp"),
        P("dp"),
    )
    return jax.shard_map(
        local,
        mesh=mesh,
        in_specs=placed,
        out_specs=(P("tensor", "dp"), P("tensor", "dp")),
        check_vma=False,
    )
```

```python
import math

import jax
import jax.numpy as jnp
from jax import lax
from jax.experimental import pallas as pl
from jax.experimental.pallas import tpu as pltpu
from jax.sharding import PartitionSpec as P

D = 16384
NEG_FILL = -1e30
MESH = pl.DeviceIdType.MESH
LOG_BASE = math.log(500000.0)
F32 = jnp.float32
BF16 = jnp.bfloat16
NY, NZ = 4, 8
CH = 512
HC = CH // 2
NCH = 4


def kernel(
    len_ref, pos_ref, q_ref, k_ref, v_ref, nk_ref, nv_ref, w_ref, res_ref, gain_ref,
    normed_ref, stream_ref,
    kbuf, vbuf, wbuf, nkbuf, nvbuf, resbuf, gainbuf, krotbuf, nvf,
    q1buf, q2buf, qf, accf, accb, statb, cbuf, sbuf, attbuf,
    ysend, ypass, yfwd, yrecv, zf, zsend, zrecv, sf, sqsend, sqrecv,
    lsem, ssem, wsem, q1sem, q2sem, csem, tsem, dsem, rsem, ysem, zsem, qsem,
):
    x = lax.axis_index("dp")
    t = lax.axis_index("tensor")
    c = lax.rem(t, 2)
    z = lax.rem(t // 2, NZ)
    y = t // (2 * NZ)
    g = t // 8
    b = lax.rem(t, 8)
    gpar = lax.rem(g, 2)
    tt = lax.rem(t, 16)

    def dev(yy, zz, cc):
        return (yy * NZ + zz) * 2 + cc

    loads = []

    def load(src, dst):
        cp = pltpu.make_async_copy(src, dst, lsem.at[len(loads)])
        cp.start()
        loads.append(cp)
        return cp

    small = [
        load(nk_ref.at[:, pl.ds(pl.multiple_of(g * 128, 128), 128)], nkbuf),
        load(nv_ref.at[:, pl.ds(pl.multiple_of(g * 128, 128), 128)], nvbuf),
    ]
    kload = [load(k_ref.at[pl.ds(8 * i, 8)], kbuf.at[pl.ds(8 * i, 8)]) for i in range(4)]
    vload = [load(v_ref.at[pl.ds(8 * i, 8)], vbuf.at[pl.ds(8 * i, 8)]) for i in range(4)]
    mycols = pl.ds(pl.multiple_of(c * (NCH * CH), NCH * CH), NCH * CH)
    theircols = pl.ds(pl.multiple_of((1 - c) * (NCH * CH), NCH * CH), NCH * CH)
    wload = [
        load(w_ref.at[pl.ds(64 * i, 64), mycols], wbuf.at[c, pl.ds(64 * i, 64)]) for i in range(4)
    ]
    late = [load(res_ref, resbuf), load(gain_ref, gainbuf)]

    barrier = pltpu.get_barrier_semaphore()
    partners = []
    for d in range(1, 16):
        partners.append((x, y * 16 + lax.rem(tt + d, 16)))
    for d in range(1, NY):
        for cc in range(2):
            partners.append((x, dev(lax.rem(y + d, NY), z, cc)))
    for d in range(1, 4):
        for cc in range(2):
            partners.append((lax.rem(x + d, 4), dev(y, z, cc)))
    for px, pt in partners:
        pl.semaphore_signal(barrier, inc=1, device_id=(px, pt), device_id_type=MESH)
    pl.semaphore_wait(barrier, len(partners))

    sends = []
    counter = [0]

    def remote(src, dst, rsem, pt, px=x, keep=True):
        cp = pltpu.make_async_remote_copy(
            src_ref=src, dst_ref=dst, send_sem=ssem.at[counter[0]], recv_sem=rsem,
            device_id=(px, pt), device_id_type=MESH,
        )
        counter[0] += 1
        if keep:
            cp.start()
            sends.append(cp)
        return cp

    def arrived(ref, sem):
        pltpu.make_async_copy(ref, ref, sem).wait()

    ydest = 2 * lax.rem(z, 2) + c
    q1 = []
    for half in range(2):
        target = dev(ydest, z, half)
        src = q_ref.at[:, half * 128:(half + 1) * 128]
        dst = q1buf.at[y]
        cp = remote(src, dst, q1sem.at[y], target, keep=False)
        here = jnp.logical_and(ydest == y, c == half)
        mine = pltpu.make_async_copy(src, dst, q1sem.at[y])
        q1.append((cp, here))

        @pl.when(here)
        def _():
            mine.start()

        @pl.when(jnp.logical_not(here))
        def _():
            cp.start()

    relay = lax.rem(z, 2) == y // 2
    slot = z // 2
    q2 = []
    for i in range(4):
        for cc in range(2):
            zz = 4 * c + lax.rem(z + i, 4)
            target = dev(y, zz, cc)
            cp = remote(q1buf, q2buf.at[slot], q2sem.at[slot], target, keep=False)
            here = jnp.logical_and(zz == z, c == cc)
            mine = pltpu.make_async_copy(q1buf, q2buf.at[slot], q2sem.at[slot])
            q2.append((cp, mine, here))

    @pl.when(relay)
    def _():
        for i in range(NY):
            arrived(q1buf.at[i], q1sem.at[i])
        for cp, mine, here in q2:
            @pl.when(here)
            def _():
                mine.start()

            @pl.when(jnp.logical_not(here))
            def _():
                cp.start()

    for i in range(4):
        remote(
            w_ref.at[pl.ds(64 * i, 64), theircols], wbuf.at[c, pl.ds(64 * i, 64)],
            wsem.at[i], dev(y, z, 1 - c),
        )

    for cp in small:
        cp.wait()
    row_ids = lax.broadcasted_iota(jnp.int32, (32, 128), 0)
    lane_ids = lax.broadcasted_iota(jnp.int32, (32, 128), 1)
    pos = jnp.zeros((32, 128), jnp.int32)
    for r in range(32):
        pos = jnp.where(row_ids == r, pos_ref[r], pos)
    j = jnp.where(lane_ids < 64, lane_ids, lane_ids - 64).astype(F32)
    frequency = jnp.exp(-(j * (2.0 / 128.0)) * LOG_BASE)
    angle = pos.astype(F32) * frequency
    cosine = jnp.cos(angle)
    sine = jnp.sin(angle)
    fresh_key = nkbuf[...].astype(F32)
    swapped = pltpu.roll(fresh_key, 64, 1)
    signed = jnp.where(lane_ids < 64, -sine, sine)
    krotbuf[...] = (fresh_key * cosine + swapped * signed).astype(BF16).astype(F32)
    nvf[...] = nvbuf[...].astype(F32)

    for cp in kload + vload:
        cp.wait()
    for i in range(4):
        arrived(q2buf.at[i], q2sem.at[i])
    for i in range(4):
        for ys in range(NY):
            qf[:, 4 * ys + i, :] = q2buf[i, ys].astype(F32)

    inv_root = 1.0 / math.sqrt(128.0)
    slot_ids = b * 512 + lax.broadcasted_iota(jnp.int32, (16, 512), 1)
    stat_lane = lax.broadcasted_iota(jnp.int32, (16, 128), 1)
    holder = b == 0
    stats = jnp.zeros((16, 128), F32)
    for ch in range(2):
        def group(i, stats, ch=ch):
            base = (ch * 2 + i) * 8
            for u in range(8):
                r = base + u
                qrow = qf[r]
                used = slot_ids < len_ref[r]
                score = lax.dot_general(
                    qrow.astype(BF16), kbuf[r], (((1,), (1,)), ((), ())),
                    preferred_element_type=F32,
                ) * inv_root
                score = jnp.where(used, score, NEG_FILL)
                fresh = jnp.sum(qrow * krotbuf[pl.ds(r, 1), :], axis=1, keepdims=True) * inv_root
                fresh = jnp.where(holder, fresh, NEG_FILL)
                top = jnp.maximum(jnp.max(score, axis=1, keepdims=True), fresh)
                weight = jnp.where(used, jnp.exp(score - top), 0.0)
                fresh_weight = jnp.where(holder, jnp.exp(fresh - top), 0.0)
                total = jnp.sum(weight, axis=1, keepdims=True) + fresh_weight
                acc = jnp.dot(weight.astype(BF16), vbuf[r], preferred_element_type=F32)
                acc = acc + fresh_weight * nvf[pl.ds(r, 1), :]
                accf[i, :, u, :] = acc
                stats = jnp.where(stat_lane == r, top, stats)
                stats = jnp.where(stat_lane == r + 64, total, stats)
            return stats

        stats = lax.fori_loop(0, 2, group, stats)
        merged = jnp.concatenate([accf[0], accf[1]], axis=1).astype(BF16)
        accb[ch] = merged.reshape(8, 2, 16, 128)
        if ch == 1:
            for o in range(8):
                statb[o] = stats[2 * o:2 * o + 2]
        for d in range(1, 8):
            o = lax.rem(b + d, 8)
            remote(accb.at[ch, o], cbuf.at[ch, d], csem.at[ch, d], g * 8 + o)
            if ch == 1:
                remote(statb.at[o], sbuf.at[d], tsem.at[d], g * 8 + o)
        cbuf[ch, 0] = accb[ch, b]
    sbuf[0] = statb[b]

    for d in range(1, 8):
        arrived(sbuf.at[d], tsem.at[d])
    rows = [sbuf[d] for d in range(8)]
    stacked = jnp.concatenate(
        [row[0:1] for row in rows] + [row[1:2] for row in rows], axis=0
    )
    turned = stacked.T
    for d in range(1, 8):
        arrived(cbuf.at[0, d], csem.at[0, d])
        arrived(cbuf.at[1, d], csem.at[1, d])
    for h in range(2):
        tops = turned[0:32, h * 8:h * 8 + 8]
        sums = turned[64:96, h * 8:h * 8 + 8]
        top = jnp.max(tops, axis=1, keepdims=True)
        scale = jnp.exp(tops - top)
        scale = scale / jnp.sum(scale * sums, axis=1, keepdims=True)
        total = jnp.zeros((32, 128), F32)
        for d in range(8):
            part = jnp.concatenate([cbuf[0, d, h], cbuf[1, d, h]], axis=0).astype(F32)
            total = total + part * scale[:, d:d + 1]
        attbuf[c, x, :, h * 128:(h + 1) * 128] = total.astype(BF16)

    for d in (2, 1, 3, 0):
        o = lax.rem(x + d, 4)
        for cc in (c, 1 - c):
            if d > 0 or cc is not c:
                remote(attbuf.at[c, x], attbuf.at[c, x], dsem.at[c, x], dev(y, z, cc), px=o)
    for cp in wload:
        cp.wait()
    for i in range(4):
        arrived(wbuf.at[1 - c, pl.ds(64 * i, 64)], wsem.at[i])
    for d in (0, 1, 3, 2):
        o = lax.rem(x + d, 4)
        for cc in (c, 1 - c):
            if d > 0 or cc is not c:
                arrived(attbuf.at[cc, o], dsem.at[cc, o])
    att = jnp.concatenate([attbuf[0].reshape(128, 256), attbuf[1].reshape(128, 256)], axis=1)

    sides = (lax.rem(y + 1, NY), lax.rem(y + 3, NY))
    opposite = lax.rem(y + 2, NY)

    def forward(i):
        for s in range(2):
            arrived(ypass.at[i, s], rsem.at[i, s])
            term = ysend[i, sides[s], s].astype(F32) + ypass[i, s].astype(F32)
            yfwd[i, s] = term.astype(BF16)
            remote(yfwd.at[i, s], yrecv.at[i, s, s], ysem.at[i, s, s], dev(sides[s], z, c))

    for i in range(NCH):
        own = jnp.dot(
            att, wbuf[:, :, i * CH:(i + 1) * CH].reshape(512, CH), preferred_element_type=F32
        ).astype(BF16)
        for s in range(2):
            ysend[i, :, s] = own[:, s * HC:(s + 1) * HC].reshape(NY, 32, HC)
        for s in range(2):
            remote(ysend.at[i, opposite, s], ypass.at[i, s], rsem.at[i, s], dev(sides[s], z, c))
        for s in range(2):
            remote(
                ysend.at[i, sides[s], 1 - s], yrecv.at[i, s, 1 - s], ysem.at[i, s, 1 - s],
                dev(sides[s], z, c),
            )
        if i > 0:
            forward(i - 1)
    forward(NCH - 1)

    for p in range(2):
        for k in range(2):
            i = 2 * p + k
            for side in range(2):
                for s in range(2):
                    arrived(yrecv.at[i, side, s], ysem.at[i, side, s])
            for s in range(2):
                summed = ysend[i, y, s].astype(F32)
                for side in range(2):
                    summed = summed + yrecv[i, side, s].astype(F32)
                for cb in range(2):
                    zf[:, 4 * k + 2 * s + cb, :] = summed[:, cb * 128:(cb + 1) * 128]
        zsend[p] = zf[...].astype(BF16).reshape(16, 2, 8, 128)
        for d in (8, 7, 9, 6, 10, 5, 11, 4, 12, 3, 13, 2, 14, 1, 15):
            o = lax.rem(tt + d, 16)
            remote(zsend.at[p, o], zrecv.at[p, d], zsem.at[p, d], y * 16 + o)
        zrecv[p, 0] = zsend[p, tt]
    for cp in late:
        cp.wait()
    for p in range(2):
        for d in range(1, 16):
            arrived(zrecv.at[p, d], zsem.at[p, d])
        for parity in range(2):
            total = zrecv[p, parity].astype(F32)
            for d in range(parity + 2, 16, 2):
                total = total + zrecv[p, d].astype(F32)
            half = c if parity == 0 else 1 - c
            for row in range(2):
                sf[row, half, p * 8:(p + 1) * 8, :] = total[row]
    hidden = jnp.concatenate(
        [sf[:, half, cb, :] for half in range(2) for cb in range(16)], axis=1
    )
    hidden = resbuf[...].astype(F32) + hidden
    stream_ref[...] = hidden.astype(BF16)
    squares = jnp.sum(hidden * hidden, axis=1, keepdims=True)
    sqsend[...] = jnp.broadcast_to(squares, (2, 128))
    for d in range(1, 4):
        remote(sqsend, sqrecv.at[d - 1], qsem.at[d - 1], t, px=lax.rem(x + d, 4))
    for d in range(1, 4):
        arrived(sqrecv.at[d - 1], qsem.at[d - 1])
    whole = sqsend[...]
    for d in range(3):
        whole = whole + sqrecv[d]
    factor = lax.rsqrt(whole[:, 0:1] / D + 1e-05)
    normed_ref[...] = (hidden * factor * gainbuf[...].astype(F32)).astype(BF16)

    for cp, here in q1:
        @pl.when(jnp.logical_not(here))
        def _():
            cp.wait_send()

    @pl.when(relay)
    def _():
        for cp, mine, here in q2:
            @pl.when(jnp.logical_not(here))
            def _():
                cp.wait_send()
    for cp in sends:
        cp.wait_send()


def local(query, cache_keys, cache_values, new_key, new_value, lengths, positions, out_weight, residual, norm_gain):
    any_spec = pl.BlockSpec(memory_space=pl.ANY)
    smem = pl.BlockSpec(memory_space=pltpu.SMEM)
    vmem = pl.BlockSpec(memory_space=pltpu.VMEM)
    dma = pltpu.SemaphoreType.DMA
    normed, stream = pl.pallas_call(
        kernel,
        out_shape=(
            jax.ShapeDtypeStruct((2, 4096), BF16),
            jax.ShapeDtypeStruct((2, 4096), BF16),
        ),
        in_specs=[smem, smem] + [any_spec] * 8,
        out_specs=(vmem, vmem),
        scratch_shapes=[
            pltpu.VMEM((32, 512, 128), BF16),
            pltpu.VMEM((32, 512, 128), BF16),
            pltpu.VMEM((2, 256, NCH * CH), BF16),
            pltpu.VMEM((32, 128), BF16),
            pltpu.VMEM((32, 128), BF16),
            pltpu.VMEM((2, 4096), BF16),
            pltpu.VMEM((1, 4096), BF16),
            pltpu.VMEM((32, 128), F32),
            pltpu.VMEM((32, 128), F32),
            pltpu.VMEM((4, 32, 128), BF16),
            pltpu.VMEM((4, 4, 32, 128), BF16),
            pltpu.VMEM((32, 16, 128), F32),
            pltpu.VMEM((2, 16, 8, 128), F32),
            pltpu.VMEM((2, 8, 2, 16, 128), BF16),
            pltpu.VMEM((8, 2, 128), F32),
            pltpu.VMEM((2, 8, 2, 16, 128), BF16),
            pltpu.VMEM((8, 2, 128), F32),
            pltpu.VMEM((2, 4, 32, 256), BF16),
            pltpu.VMEM((NCH, 4, 2, 32, HC), BF16),
            pltpu.VMEM((NCH, 2, 32, HC), BF16),
            pltpu.VMEM((NCH, 2, 32, HC), BF16),
            pltpu.VMEM((NCH, 2, 2, 32, HC), BF16),
            pltpu.VMEM((32, 8, 128), F32),
            pltpu.VMEM((2, 16, 2, 8, 128), BF16),
            pltpu.VMEM((2, 16, 2, 8, 128), BF16),
            pltpu.VMEM((2, 2, 16, 128), F32),
            pltpu.VMEM((2, 128), F32),
            pltpu.VMEM((3, 2, 128), F32),
            dma((16,)),
            dma((112,)),
            dma((4,)),
            dma((4,)),
            dma((4,)),
            dma((2, 8)),
            dma((8,)),
            dma((2, 4)),
            dma((NCH, 2)),
            dma((NCH, 2, 2)),
            dma((2, 16)),
            dma((3,)),
        ],
        compiler_params=pltpu.CompilerParams(
            collective_id=0, has_side_effects=True, vmem_limit_bytes=60 * 1024 * 1024
        ),
    )(
        lengths, positions, query, cache_keys, cache_values, new_key, new_value,
        out_weight, residual, norm_gain.reshape(1, -1),
    )
    return normed, stream


def solution(mesh):
    placed = (
        P("dp", "tensor"),
        P("dp", "tensor", None),
        P("dp", "tensor", None),
        P("dp", None),
        P("dp", None),
        P("dp"),
        P("dp"),
        P("tensor", "dp"),
        P("tensor", "dp"),
        P("dp"),
    )
    return jax.shard_map(
        local,
        mesh=mesh,
        in_specs=placed,
        out_specs=(P("tensor", "dp"), P("tensor", "dp")),
        check_vma=False,
    )
```
